32 devices in a mesh: groups: 1, tile: 32 (over z, y, x, core).
Axes of the slice: x: 2, y: 2, z: 4, core: 2. Of those that a mesh axis runs over, the one named last changes fastest.
Arguments:
- tiles: bfloat16 [256, 64, 2048], P(('groups', 'tile')), may hold values from -6 to 6
- slide_of: int32 [256], P(('groups', 'tile')), may hold values from 0 to 3, as said below
- valid_count: int32 [32], P(('groups', 'tile')), may hold values from 1 to 8, as said below
- labels: int32 [4], P('groups'), may hold values from 0 to 1
- w_reduce: bfloat16 [2048, 1024], replicated, may hold values from -0.125 to 0.125
- w_expand: bfloat16 [1024, 2048], replicated, may hold values from -0.1875 to 0.1875
- queries: bfloat16 [64, 2048], replicated, may hold values from -16 to 16
- cls_weight: bfloat16 [64, 2048], replicated, may hold values from -0.0625 to 0.0625
Outputs:
- slide_loss: float32 [4], P('groups')
- d_queries: float32 [64, 2048], P('groups')
- d_reduce: float32 [2048, 1024], P(('groups', 'tile'))
- d_expand_t: float32 [2048, 1024], P(('groups', 'tile'))
The draws below stay inside these ranges and needn't reach their ends.
Inputs may be any that keep to these rules, and one draw needn't show every extreme that they name: `slide_of`: every slide has a valid tile. `valid_count`: some device has all 8 slots valid.
All inputs are finite; a program needn't handle non-finite values.
Results may differ from the reference program's by a relative error of at most 0.0039.
Values sent between devices are 32-bit elements; how exact they have to be, the bound alone decides.
A program may use at most 192 MiB of HBM per device.

```python
import jax
import jax.numpy as jnp
from jax import lax

D = 2048
MID = 1024
POS = 64
QUERIES = 64
TILE_DEV = 8
SLIDES = 4
TILES = 256


def draw_slide_of(key, part):
    places = jnp.arange(TILES).astype(jnp.int32)
    picked = jax.random.randint(key, (TILES,), 0, SLIDES).astype(jnp.int32)
    first = places // TILE_DEV % SLIDES
    return jnp.where(places % TILE_DEV == 0, first, picked).astype(jnp.int32)


def draw_valid_count(key, part):
    devices_here = TILES // TILE_DEV
    first_key = jax.random.fold_in(key, 11)
    second_key = jax.random.fold_in(key, 23)
    counts = jax.random.randint(first_key, (devices_here,), 1, TILE_DEV + 1).astype(jnp.int32)
    chosen = jax.random.randint(second_key, (), 0, devices_here).astype(jnp.int32)
    return jnp.where(jnp.arange(devices_here).astype(jnp.int32) == chosen, TILE_DEV, counts).astype(jnp.int32)


def draw_queries(key, part):
    base = jax.random.normal(key, (QUERIES, D), jnp.float32)
    return jnp.clip(base, -6.0, 6.0).astype(jnp.bfloat16)


def with_ends(values, own_key, smallest, top_value):
    spot = [jax.random.randint(jax.random.fold_in(own_key, axis), (), 0, length) for axis, length in enumerate(values.shape)]
    widest = values.shape.index(max(values.shape))
    neighbour = spot[:widest] + [(spot[widest] + 1) % values.shape[widest]] + spot[widest + 1:]
    return values.at[tuple(spot)].set(smallest).at[tuple(neighbour)].set(top_value)


def with_spikes(drawn, own_key, source, target, blocks, factor):
    owner, partner = [(jnp.arange(drawn.shape[axis_at]) // (drawn.shape[axis_at] // blocks)).reshape([-1 if axis == axis_at else 1 for axis in range(drawn.ndim)]) for axis_at in (source, target)]
    chosen = jax.random.permutation(own_key, blocks)[partner]
    strong = (owner == chosen) | (owner == (partner + blocks // 2) % blocks)
    return jnp.where(strong, factor * drawn, drawn)


def steps_of(rng, dims, shards, low, top_value):
    loudness = 1.0
    for dim, blocks in shards:
        steps = jax.random.uniform(jax.random.fold_in(jax.random.fold_in(rng, 6), dim), (blocks,), jnp.float32, low / len(shards), top_value / len(shards))
        loudness = loudness * jnp.repeat(jnp.exp(steps), dims[dim] // blocks).reshape((-1,) + (1,) * (len(dims) - 1 - dim))
    return loudness


def noise(rng, extent, width, bound, cuts=(), held_as=jnp.bfloat16):
    result = width * jax.random.normal(rng, extent, jnp.float32)
    if cuts:
        result = result * steps_of(rng, extent, cuts, -0.22, 0.18)
    return jnp.clip(result, -bound, bound).astype(held_as)


def noise_with(rng, extent, spread, bound, split, heavy, held_as=jnp.bfloat16):
    entries = spread * jax.random.normal(rng, extent, jnp.float32)
    if split:
        entries = entries * steps_of(rng, extent, split, -0.22, 0.18)
    return jnp.clip(with_spikes(entries, jax.random.fold_in(rng, 3), *heavy), -bound, bound).astype(held_as)


def setup_inputs(seed: int = 0, part: int = 0) -> dict:
    arg_keys = jax.random.split(jax.random.key(seed), 9)
    part_splits = jax.random.split(jax.random.fold_in(arg_keys[8], part), 9)
    return {
        "tiles": noise_with(part_splits[0], (TILES, POS, D), 1.0, 6.0, ((0, 32),), (0, 2, 32, 2.75)),
        "slide_of": draw_slide_of(jax.random.fold_in(jax.random.fold_in(arg_keys[8], part), 71), part),
        "valid_count": draw_valid_count(jax.random.fold_in(jax.random.fold_in(arg_keys[8], part), 71), part),
        "labels": with_ends(jax.random.randint(part_splits[3], (SLIDES,), 0, 2), jax.random.fold_in(part_splits[3], 1), 0, 1).astype(jnp.int32),
        "w_reduce": noise(arg_keys[4], (D, MID), D ** -0.5, 0.125),
        "w_expand": noise(arg_keys[5], (MID, D), MID ** -0.5, 0.1875),
        "queries": draw_queries(jax.random.fold_in(arg_keys[8], 71), part),
        "cls_weight": noise(arg_keys[7], (QUERIES, D), (QUERIES * D // 16) ** -0.5, 0.0625),
    }


HIGH = lax.Precision.HIGHEST

def slope(values):
    sig = jax.nn.sigmoid(values)
    return sig * (1.0 + values * (1.0 - sig))

def encode(block, w_reduce, w_expand):
    tile_rows = block.reshape(-1, D)
    pre_mid = jnp.dot(tile_rows, w_reduce, preferred_element_type=jnp.float32)
    hidden_act = jax.nn.silu(pre_mid).astype(jnp.bfloat16)
    pre_out = tile_rows.astype(jnp.float32) + jnp.dot(hidden_act, w_expand, preferred_element_type=jnp.float32)
    return (tile_rows, pre_mid, hidden_act, pre_out)

def reference(tiles, slide_of, valid_count, labels, w_reduce, w_expand, queries, cls_weight):
    blocks = tiles.reshape(-1, TILE_DEV, POS, D)

    def embed_block(block):
        pre_out = encode(block, w_reduce, w_expand)[3]
        return jax.nn.silu(pre_out).reshape(TILE_DEV, POS, D).mean(axis=1)
    embed = lax.map(embed_block, blocks).reshape(-1, D)
    places = jnp.arange(TILES).astype(jnp.int32)
    valid = places % TILE_DEV < valid_count[places // TILE_DEV]
    member = ((slide_of[:, None] == jnp.arange(SLIDES).astype(jnp.int32)[None, :]) & valid[:, None]).astype(jnp.float32)
    query_vals = queries.astype(jnp.float32)
    inv_root = 1.0 / jnp.sqrt(jnp.float32(D))
    scores = jnp.dot(embed, query_vals.T, precision=HIGH) * inv_root
    top_scores = lax.optimization_barrier(jnp.max(jnp.where(member[:, :, None] > 0, scores[:, None, :], -1e+30), axis=0))
    tile_top = jnp.dot(member, top_scores, precision=HIGH)
    weights = jnp.where(valid[:, None], jnp.exp(jnp.where(valid[:, None], scores - tile_top, 0.0)), 0.0)
    totals = jnp.dot(member.T, weights, precision=HIGH)
    numerators = jnp.einsum('ts,tq,td->sqd', member, weights, embed, precision=HIGH)
    pooled = numerators / totals[:, :, None]
    class_vals = cls_weight.astype(jnp.float32)
    logit = lax.optimization_barrier(jnp.sum(pooled * class_vals[None], axis=(1, 2)))
    targets = labels.astype(jnp.float32)
    slide_loss = jax.nn.softplus(logit) - targets * logit
    dlogit = (jax.nn.sigmoid(logit) - targets) / SLIDES
    dpooled = dlogit[:, None, None] * class_vals[None]
    tile_totals = jnp.where(valid[:, None], jnp.dot(member, totals, precision=HIGH), 1.0)
    prob = weights / tile_totals
    grad_dot = jnp.einsum('ts,sqd,td->tq', member, dpooled, embed, precision=HIGH)
    pooled_dot = lax.optimization_barrier(jnp.sum(dpooled * pooled, axis=2))
    dscore = prob * (grad_dot - jnp.dot(member, pooled_dot, precision=HIGH))
    dembed = jnp.dot(dscore, query_vals, precision=HIGH) * inv_root + jnp.einsum('ts,tq,sqd->td', member, prob, dpooled, precision=HIGH)
    d_queries = jnp.dot(dscore.T, embed, precision=HIGH) * inv_root
    dembed_blocks = dembed.reshape(-1, TILE_DEV, D)

    def advance(acc_pair, pieces):
        block, block_grad = pieces
        tile_rows, pre_mid, hidden_act, pre_out = encode(block, w_reduce, w_expand)
        dout = slope(pre_out).reshape(TILE_DEV, POS, D) * (block_grad[:, None, :] / POS)
        dout = dout.reshape(-1, D).astype(jnp.bfloat16)
        dmid = jnp.dot(dout, w_expand.T, preferred_element_type=jnp.float32)
        dpre_mid = (dmid * slope(pre_mid)).astype(jnp.bfloat16)
        grad_red = acc_pair[0] + jnp.dot(tile_rows.T, dpre_mid, preferred_element_type=jnp.float32)
        grad_exp = acc_pair[1] + jnp.dot(dout.T, hidden_act, preferred_element_type=jnp.float32)
        return ((grad_red, grad_exp), None)
    zeros_pair = (jnp.zeros((D, MID), jnp.float32), jnp.zeros((D, MID), jnp.float32))
    grads_pair, _ = lax.scan(advance, zeros_pair, (blocks, dembed_blocks))
    return (slide_loss, d_queries, grads_pair[0], grads_pair[1])
```

```python
import jax
import jax.numpy as jnp
from jax import lax
from jax.sharding import PartitionSpec as P

HIGH = lax.Precision.HIGHEST


def slope(values):
    sig = jax.nn.sigmoid(values)
    return sig * (1.0 + values * (1.0 - sig))


def on_device(tiles, slide_of, valid_count, labels, w_reduce, w_expand, queries, cls_weight):
    count_tiles, positions, width = tiles.shape
    slides = labels.shape[0]
    tile_rows = tiles.reshape(-1, width)
    pre_mid = jnp.dot(tile_rows, w_reduce, preferred_element_type=jnp.float32)
    hidden_act = jax.nn.silu(pre_mid).astype(jnp.bfloat16)
    pre_out = tile_rows.astype(jnp.float32) + jnp.dot(
        hidden_act, w_expand, preferred_element_type=jnp.float32
    )
    embed = jax.nn.silu(pre_out).reshape(count_tiles, positions, width).mean(axis=1)
    valid = jnp.arange(count_tiles) < valid_count[0]
    member = ((slide_of[:, None] == jnp.arange(slides)[None, :]) & valid[:, None]).astype(
        jnp.float32
    )
    query_vals = queries.astype(jnp.float32)
    class_vals = cls_weight.astype(jnp.float32)
    inv_root = 1.0 / jnp.sqrt(jnp.float32(width))
    count_queries = query_vals.shape[0]
    both_vals = jnp.concatenate([query_vals * inv_root, class_vals], axis=0)
    both = jnp.dot(embed, both_vals.T, precision=HIGH)
    scores = both[:, :count_queries]
    class_dot = both[:, count_queries:]
    of_slide = member[:, :, None]

    def per_tile(slide_vals):
        return jnp.sum(of_slide * slide_vals[None], axis=1)

    local_top = jnp.max(jnp.where(of_slide > 0, scores[:, None, :], -1e30), axis=0)
    local_weights = jnp.where(
        valid[:, None], jnp.exp(jnp.where(valid[:, None], scores - per_tile(local_top), 0.0)), 0.0
    )
    part_totals = jnp.sum(of_slide * local_weights[:, None, :], axis=0)
    part_dots = jnp.sum(of_slide * (local_weights * class_dot)[:, None, :], axis=0)
    gathered = lax.all_gather(jnp.stack([local_top, part_totals, part_dots]), "tile")
    top_scores = jnp.max(gathered[:, 0], axis=0)
    rescale = jnp.exp(gathered[:, 0] - top_scores[None])
    totals = jnp.sum(rescale * gathered[:, 1], axis=0)
    ratio = jnp.sum(rescale * gathered[:, 2], axis=0) / totals
    logit = jnp.sum(ratio, axis=1)
    targets = labels.astype(jnp.float32)
    slide_loss = jax.nn.softplus(logit) - targets * logit
    dlogit = (jax.nn.sigmoid(logit) - targets) / slides
    weights = jnp.where(
        valid[:, None], jnp.exp(jnp.where(valid[:, None], scores - per_tile(top_scores), 0.0)), 0.0
    )
    prob = weights / jnp.where(valid[:, None], per_tile(totals), 1.0)
    prob_grad = prob * jnp.sum(member * dlogit[None], axis=1)[:, None]
    dscore = prob_grad * (class_dot - per_tile(ratio))
    dembed = jnp.dot(
        jnp.concatenate([dscore, prob_grad], axis=1), both_vals, precision=HIGH
    )
    query_terms = jnp.dot(dscore.T, embed, precision=HIGH) * inv_root
    d_queries = lax.psum(query_terms, "tile")
    dout = slope(pre_out).reshape(count_tiles, positions, width) * (dembed[:, None, :] / positions)
    dout = dout.reshape(-1, width).astype(jnp.bfloat16)
    dmid = jnp.dot(dout, w_expand.T, preferred_element_type=jnp.float32)
    dpre_mid = (dmid * slope(pre_mid)).astype(jnp.bfloat16)
    stacked = lax.psum_scatter(
        jnp.concatenate(
            [
                jnp.einsum("rc,rm->cm", tile_rows, dpre_mid, preferred_element_type=jnp.float32),
                jnp.einsum("rc,rm->cm", dout, hidden_act, preferred_element_type=jnp.float32),
            ],
            axis=1,
        ),
        "tile",
        scatter_dimension=0,
        tiled=True,
    )
    middle = hidden_act.shape[1]
    d_reduce = stacked[:, :middle]
    d_expand_t = stacked[:, middle:]
    return (slide_loss, d_queries, d_reduce, d_expand_t)


def solution(mesh):
    return jax.shard_map(
        on_device,
        mesh=mesh,
        in_specs=(
            P(("groups", "tile"), None, None),
            P(("groups", "tile")),
            P(("groups", "tile")),
            P("groups"),
            P(),
            P(),
            P(),
            P(),
        ),
        out_specs=(
            P("groups"),
            P("groups", None),
            P(("groups", "tile"), None),
            P(("groups", "tile"), None),
        ),
        check_vma=False,
    )
```

```python
import functools

import jax
import jax.numpy as jnp
from jax import lax
from jax.experimental import pallas as pl
from jax.experimental.pallas import tpu as pltpu
from jax.sharding import PartitionSpec as P

HIGH = lax.Precision.HIGHEST


def slope(values):
    sig = jax.nn.sigmoid(values)
    return sig * (1.0 + values * (1.0 - sig))


def bit_orders(count):
    bits = count.bit_length() - 1
    ring = list(range(1, bits))
    if bits != 5:
        return [[0] + ring[r:] + ring[:r] for r in (0, 1, 2)]
    return [[0, 1, 2, 3, 4], [0, 2, 1, 3, 4], [0, 3, 4, 1, 2]]


def place_of(block, order):
    place = 0
    for bit in order:
        place = place * 2 + (block // (1 << bit)) % 2
    return place


def reduce_kernel(count, orders, widths, tiles_ref, dmid_ref, dout_ref, hidden_ref, query_ref,
                  red_ref, exp_ref, query_out_ref, *scratch):
    rounds = 2
    kinds = len(orders)
    grads = scratch[:rounds * kinds]
    lands = scratch[rounds * kinds:2 * rounds * kinds]
    query_sum, query_land, send_sem, recv_sem, query_send, query_recv = scratch[2 * rounds * kinds:]
    steps = len(orders[0])
    me = lax.axis_index("tile")
    rows = tiles_ref.shape[1] // count
    query_rows = query_ref.shape[0] // count

    partners = [me + (1 << bit) * (1 - 2 * ((me // (1 << bit)) % 2)) for bit in range(steps)]
    barrier = pltpu.get_barrier_semaphore()
    for bit in range(steps):
        pl.semaphore_signal(barrier, inc=1, device_id={"tile": partners[bit]},
                            device_id_type=pl.DeviceIdType.MESH)
    pl.semaphore_wait(barrier, steps)

    def span(order, step, unit):
        half = count >> (step + 1)
        base = 0
        for at in range(step):
            base = base + ((me // (1 << order[at])) % 2) * (count >> (at + 1))
        mine = (me // (1 << order[step])) % 2
        keep = pl.multiple_of((base + mine * half) * unit, unit)
        give = pl.multiple_of((base + (1 - mine) * half) * unit, unit)
        return keep, give, half * unit

    def land_at(step, unit):
        return (count - (count >> step)) * unit

    def begin(source, land, order, step, unit, sends, recvs):
        keep, give, size = span(order, step, unit)
        copy = pltpu.make_async_remote_copy(
            src_ref=source.at[pl.ds(give, size)],
            dst_ref=land.at[pl.ds(land_at(step, unit), size)],
            send_sem=sends, recv_sem=recvs,
            device_id={"tile": partners[order[step]]},
            device_id_type=pl.DeviceIdType.MESH,
        )
        copy.start()
        return copy

    def add(source, land, order, step, unit):
        keep, give, size = span(order, step, unit)
        piece = min(size, 64)

        @pl.loop(0, size // piece)
        def _(at):
            here = pl.ds(pl.multiple_of(keep + at * piece, piece), piece)
            there = pl.ds(pl.multiple_of(land_at(step, unit) + at * piece, piece), piece)
            source[here, :] = source[here, :] + land[there, :]

    query_order = orders[0]
    query_sum[...] = query_ref[...]
    query_copies = [begin(query_sum, query_land, query_order, 0, query_rows,
                          query_send.at[0], query_recv.at[0])]

    copies = [[None] * (rounds * kinds) for _ in range(steps)]
    wide = 256
    per_wide = wide // rows
    for chunk in range(rounds * kinds):
        order = orders[chunk % kinds]
        left_ref, right_ref = ((dout_ref, hidden_ref), (tiles_ref, dmid_ref))[chunk // kinds]
        first = sum(widths[:chunk % kinds])
        width = widths[chunk % kinds]

        @pl.loop(0, tiles_ref.shape[1] // wide)
        def _(at):
            product = lax.dot_general(
                left_ref[:, pl.ds(pl.multiple_of(at * wide, wide), wide)],
                right_ref[:, first:first + width],
                (((0,), (0,)), ((), ())),
                preferred_element_type=jnp.float32,
            )
            for inner in range(per_wide):
                place = place_of(at * per_wide + inner, order)
                grads[chunk][pl.ds(pl.multiple_of(place * rows, rows), rows), :] = (
                    product[inner * rows:(inner + 1) * rows, :]
                )

        copies[0][chunk] = begin(grads[chunk], lands[chunk], order, 0, rows,
                                 send_sem.at[0, chunk], recv_sem.at[0, chunk])

    for step in range(1, steps + 1):
        query_copies[step - 1].wait()
        add(query_sum, query_land, query_order, step - 1, query_rows)
        if step < steps:
            query_copies.append(begin(query_sum, query_land, query_order, step, query_rows,
                                      query_send.at[step], query_recv.at[step]))
        for chunk in range(rounds * kinds):
            order = orders[chunk % kinds]
            copies[step - 1][chunk].wait()
            add(grads[chunk], lands[chunk], order, step - 1, rows)
            if step < steps:
                copies[step][chunk] = begin(grads[chunk], lands[chunk], order, step, rows,
                                            send_sem.at[step, chunk], recv_sem.at[step, chunk])
            else:
                place = place_of(me, order)
                first = sum(widths[:chunk % kinds])
                out_ref = (exp_ref, red_ref)[chunk // kinds]
                out_ref[:, first:first + widths[chunk % kinds]] = grads[chunk][
                    pl.ds(pl.multiple_of(place * rows, rows), rows), :
                ]

    place = place_of(me, query_order)
    own = pl.ds(pl.multiple_of(place * query_rows, query_rows), query_rows)
    query_out_ref[own, :] = query_sum[own, :]
    for step in reversed(range(steps)):
        keep, give, size = span(query_order, step, query_rows)
        held = query_out_ref.at[pl.ds(keep, size)]
        copy = pltpu.make_async_remote_copy(
            src_ref=held, dst_ref=held,
            send_sem=query_send.at[steps + step], recv_sem=query_recv.at[steps + step],
            device_id={"tile": partners[query_order[step]]},
            device_id_type=pl.DeviceIdType.MESH,
        )
        copy.start()
        copy.wait()


def summed_grads(count, tile_rows, dpre_mid, dout, hidden_act, query_terms):
    width = tile_rows.shape[1]
    middle = hidden_act.shape[1]
    orders = bit_orders(count)
    steps = len(orders[0])
    widths = [3 * middle // 8, 3 * middle // 8, middle // 4]
    chunks = [w for _ in range(2) for w in widths]
    flat = query_terms.reshape(-1, 128)
    vmem = pl.BlockSpec(memory_space=pltpu.VMEM)
    return pl.pallas_call(
        functools.partial(reduce_kernel, count, orders, widths),
        out_shape=(
            jax.ShapeDtypeStruct((width // count, middle), jnp.float32),
            jax.ShapeDtypeStruct((width // count, middle), jnp.float32),
            jax.ShapeDtypeStruct(flat.shape, jnp.float32),
        ),
        in_specs=[vmem] * 5,
        out_specs=(vmem, vmem, vmem),
        scratch_shapes=(
            [pltpu.VMEM((width, w), jnp.float32) for w in chunks]
            + [pltpu.VMEM((width, w), jnp.float32) for w in chunks]
            + [
                pltpu.VMEM(flat.shape, jnp.float32),
                pltpu.VMEM(flat.shape, jnp.float32),
                pltpu.SemaphoreType.DMA((steps, len(chunks))),
                pltpu.SemaphoreType.DMA((steps, len(chunks))),
                pltpu.SemaphoreType.DMA((2 * steps,)),
                pltpu.SemaphoreType.DMA((2 * steps,)),
            ]
        ),
        compiler_params=pltpu.CompilerParams(
            collective_id=0, has_side_effects=True, vmem_limit_bytes=56 * 1024 * 1024
        ),
    )(tile_rows, dpre_mid, dout, hidden_act, flat)


def on_device(count, tiles, slide_of, valid_count, labels, w_reduce, w_expand, queries, cls_weight):
    count_tiles, positions, width = tiles.shape
    slides = labels.shape[0]
    tile_rows = tiles.reshape(-1, width)
    pre_mid = jnp.dot(tile_rows, w_reduce, preferred_element_type=jnp.float32)
    hidden_act = jax.nn.silu(pre_mid).astype(jnp.bfloat16)
    pre_out = tile_rows.astype(jnp.float32) + jnp.dot(
        hidden_act, w_expand, preferred_element_type=jnp.float32
    )
    embed = jax.nn.silu(pre_out).reshape(count_tiles, positions, width).mean(axis=1)
    valid = jnp.arange(count_tiles) < valid_count[0]
    member = ((slide_of[:, None] == jnp.arange(slides)[None, :]) & valid[:, None]).astype(
        jnp.float32
    )
    query_vals = queries.astype(jnp.float32)
    class_vals = cls_weight.astype(jnp.float32)
    inv_root = 1.0 / jnp.sqrt(jnp.float32(width))
    count_queries = query_vals.shape[0]
    both_vals = jnp.concatenate([query_vals * inv_root, class_vals], axis=0)
    both = jnp.dot(embed, both_vals.T, precision=HIGH)
    scores = both[:, :count_queries]
    class_dot = both[:, count_queries:]
    of_slide = member[:, :, None]

    def per_tile(slide_vals):
        return jnp.sum(of_slide * slide_vals[None], axis=1)

    local_top = jnp.max(jnp.where(of_slide > 0, scores[:, None, :], -1e30), axis=0)
    local_weights = jnp.where(
        valid[:, None], jnp.exp(jnp.where(valid[:, None], scores - per_tile(local_top), 0.0)), 0.0
    )
    part_totals = jnp.sum(of_slide * local_weights[:, None, :], axis=0)
    part_dots = jnp.sum(of_slide * (local_weights * class_dot)[:, None, :], axis=0)
    gathered = lax.all_gather(jnp.stack([local_top, part_totals, part_dots]), "tile")
    top_scores = jnp.max(gathered[:, 0], axis=0)
    rescale = jnp.exp(gathered[:, 0] - top_scores[None])
    totals = jnp.sum(rescale * gathered[:, 1], axis=0)
    ratio = jnp.sum(rescale * gathered[:, 2], axis=0) / totals
    logit = jnp.sum(ratio, axis=1)
    targets = labels.astype(jnp.float32)
    slide_loss = jax.nn.softplus(logit) - targets * logit
    dlogit = (jax.nn.sigmoid(logit) - targets) / slides
    weights = jnp.where(
        valid[:, None], jnp.exp(jnp.where(valid[:, None], scores - per_tile(top_scores), 0.0)), 0.0
    )
    prob = weights / jnp.where(valid[:, None], per_tile(totals), 1.0)
    prob_grad = prob * jnp.sum(member * dlogit[None], axis=1)[:, None]
    dscore = prob_grad * (class_dot - per_tile(ratio))
    dembed = jnp.dot(
        jnp.concatenate([dscore, prob_grad], axis=1), both_vals, precision=HIGH
    )
    query_terms = jnp.dot(dscore.T, embed, precision=HIGH) * inv_root
    dout = slope(pre_out).reshape(count_tiles, positions, width) * (dembed[:, None, :] / positions)
    dout = dout.reshape(-1, width).astype(jnp.bfloat16)
    dmid = jnp.dot(dout, w_expand.T, preferred_element_type=jnp.float32)
    dpre_mid = (dmid * slope(pre_mid)).astype(jnp.bfloat16)
    d_reduce, d_expand_t, d_queries = summed_grads(
        count, tile_rows, dpre_mid, dout, hidden_act, query_terms
    )
    d_queries = d_queries.reshape(query_terms.shape)
    return (slide_loss, d_queries, d_reduce, d_expand_t)


def solution(mesh):
    return jax.shard_map(
        functools.partial(on_device, mesh.shape["tile"]),
        mesh=mesh,
        in_specs=(
            P(("groups", "tile"), None, None),
            P(("groups", "tile")),
            P(("groups", "tile")),
            P("groups"),
            P(),
            P(),
            P(),
            P(),
        ),
        out_specs=(
            P("groups"),
            P("groups", None),
            P(("groups", "tile"), None),
            P(("groups", "tile"), None),
        ),
        check_vma=False,
    )
```

```python
import functools

import jax
import jax.numpy as jnp
from jax import lax
from jax.experimental import pallas as pl
from jax.experimental.pallas import tpu as pltpu
from jax.sharding import PartitionSpec as P

HIGH = lax.Precision.HIGHEST


def slope(values):
    sig = jax.nn.sigmoid(values)
    return sig * (1.0 + values * (1.0 - sig))


CHUNK = 128
LAG = 5
KINDS = (0, 1, 2, 0, 1, 2, 0, 1)


def bit_orders(count):
    bits = count.bit_length() - 1
    ring = list(range(1, bits))
    if bits != 5:
        return [[0] + ring[r:] + ring[:r] for r in (0, 1, 2)]
    return [[0, 1, 2, 3, 4], [0, 2, 1, 3, 4], [0, 3, 4, 1, 2]]


def gather_kernel(count, part_ref, all_ref, send_sem, recv_sem):
    me = lax.axis_index("tile")
    barrier = pltpu.get_barrier_semaphore()

    @pl.loop(1, count)
    def _(hop):
        pl.semaphore_signal(barrier, inc=1, device_id={"tile": lax.rem(me + hop, count)},
                            device_id_type=pl.DeviceIdType.MESH)

    all_ref[me] = part_ref[...]
    pl.semaphore_wait(barrier, count - 1)

    def copy_of(hop, slot):
        return pltpu.make_async_remote_copy(
            src_ref=part_ref, dst_ref=all_ref.at[slot],
            send_sem=send_sem.at[hop], recv_sem=recv_sem.at[hop],
            device_id={"tile": lax.rem(me + hop, count)},
            device_id_type=pl.DeviceIdType.MESH,
        )

    @pl.loop(1, count)
    def _(hop):
        copy_of(hop, me).start()

    @pl.loop(1, count)
    def _(hop):
        copy_of(hop, lax.rem(me - hop + count, count)).wait_recv()

    @pl.loop(1, count)
    def _(hop):
        copy_of(hop, me).wait_send()


def gather_parts(count, part):
    vmem = pl.BlockSpec(memory_space=pltpu.VMEM)
    rows, lanes = part.shape
    padded = jnp.pad(part, ((0, -rows % 8), (0, -lanes % 128)))
    return pl.pallas_call(
        functools.partial(gather_kernel, count),
        out_shape=jax.ShapeDtypeStruct((count,) + padded.shape, jnp.float32),
        in_specs=[vmem],
        out_specs=vmem,
        scratch_shapes=[pltpu.SemaphoreType.DMA((count,)), pltpu.SemaphoreType.DMA((count,))],
        compiler_params=pltpu.CompilerParams(collective_id=1, has_side_effects=True),
    )(padded)[:, :rows, :lanes]


def place_of(block, order):
    place = 0
    for bit in order:
        place = place * 2 + (block // (1 << bit)) % 2
    return place


def reduce_kernel(count, orders, tiles_ref, dmid_ref, dout_ref, hidden_ref, query_ref,
                  red_ref, exp_ref, query_out_ref, *scratch):
    per_matrix = hidden_ref.shape[1] // CHUNK
    chunks = 2 * per_matrix
    grads = scratch[:chunks]
    lands = scratch[chunks:2 * chunks]
    query_sum, query_land, send_sem, recv_sem, query_send, query_recv = scratch[2 * chunks:]
    steps = len(orders[0])
    me = lax.axis_index("tile")
    rows = tiles_ref.shape[1] // count
    query_rows = query_ref.shape[0] // count

    partners = [me + (1 << bit) * (1 - 2 * ((me // (1 << bit)) % 2)) for bit in range(steps)]
    barrier = pltpu.get_barrier_semaphore()
    for bit in range(steps):
        pl.semaphore_signal(barrier, inc=1, device_id={"tile": partners[bit]},
                            device_id_type=pl.DeviceIdType.MESH)
    pl.semaphore_wait(barrier, steps)

    def span(order, step, unit):
        half = count >> (step + 1)
        base = 0
        for at in range(step):
            base = base + ((me // (1 << order[at])) % 2) * (count >> (at + 1))
        mine = (me // (1 << order[step])) % 2
        keep = pl.multiple_of((base + mine * half) * unit, unit)
        give = pl.multiple_of((base + (1 - mine) * half) * unit, unit)
        return keep, give, half * unit

    def land_at(step, unit):
        return (count - (count >> step)) * unit

    def begin(source, land, order, step, unit, sends, recvs):
        keep, give, size = span(order, step, unit)
        copy = pltpu.make_async_remote_copy(
            src_ref=source.at[pl.ds(give, size)],
            dst_ref=land.at[pl.ds(land_at(step, unit), size)],
            send_sem=sends, recv_sem=recvs,
            device_id={"tile": partners[order[step]]},
            device_id_type=pl.DeviceIdType.MESH,
        )
        copy.start()
        return copy

    def add(source, land, order, step, unit):
        keep, give, size = span(order, step, unit)
        piece = min(size, 256)

        @pl.loop(0, size // piece)
        def _(at):
            here = pl.ds(pl.multiple_of(keep + at * piece, piece), piece)
            there = pl.ds(pl.multiple_of(land_at(step, unit) + at * piece, piece), piece)
            source[here, :] = source[here, :] + land[there, :]

    query_order = orders[0]
    query_sum[...] = query_ref[...]
    query_copies = [begin(query_sum, query_land, query_order, 0, query_rows,
                          query_send.at[0], query_recv.at[0])]

    def share(step):
        keep, give, size = span(query_order, step, query_rows)
        held = query_out_ref.at[pl.ds(keep, size)]
        copy = pltpu.make_async_remote_copy(
            src_ref=held, dst_ref=held,
            send_sem=query_send.at[steps + step], recv_sem=query_recv.at[steps + step],
            device_id={"tile": partners[query_order[step]]},
            device_id_type=pl.DeviceIdType.MESH,
        )
        copy.start()
        return copy

    def advance_query():
        done = len(query_copies) - 1
        query_copies[done].wait()
        if done < steps:
            add(query_sum, query_land, query_order, done, query_rows)
        if done < steps - 1:
            query_copies.append(begin(query_sum, query_land, query_order, done + 1, query_rows,
                                      query_send.at[done + 1], query_recv.at[done + 1]))
            return
        if done == steps - 1:
            own = pl.ds(pl.multiple_of(place_of(me, query_order) * query_rows, query_rows),
                        query_rows)
            query_out_ref[own, :] = query_sum[own, :]
        query_copies.append(share(2 * steps - 2 - done) if done < 2 * steps - 1 else None)

    def order_of(chunk):
        return orders[KINDS[chunk % len(KINDS)]]

    copies = {}

    def send(step, chunk):
        copies[step, chunk] = begin(grads[chunk], lands[chunk], order_of(chunk), step, rows,
                                    send_sem.at[step, chunk], recv_sem.at[step, chunk])

    wide = 256
    per_wide = wide // rows
    for matrix, (left_ref, right_ref) in enumerate(((dout_ref, hidden_ref), (tiles_ref, dmid_ref))):

        @pl.loop(0, tiles_ref.shape[1] // wide)
        def _(at):
            product = lax.dot_general(
                left_ref[:, pl.ds(pl.multiple_of(at * wide, wide), wide)],
                right_ref[...],
                (((0,), (0,)), ((), ())),
                preferred_element_type=jnp.float32,
            )
            for inner in range(per_wide):
                for kind in range(len(orders)):
                    place = place_of(at * per_wide + inner, orders[kind])
                    there = pl.ds(pl.multiple_of(place * rows, rows), rows)
                    for part in range(per_matrix):
                        if KINDS[part % len(KINDS)] == kind:
                            grads[matrix * per_matrix + part][there, :] = product[
                                inner * rows:(inner + 1) * rows, part * CHUNK:(part + 1) * CHUNK
                            ]

        for part in range(per_matrix):
            send(0, matrix * per_matrix + part)

    visits = sorted(
        ((step, chunk) for step in range(1, steps + 1) for chunk in range(chunks)),
        key=lambda visit: (visit[1] + LAG * visit[0], visit[1]),
    )
    every = len(visits) // (2 * steps)
    for at, (step, chunk) in enumerate(visits):
        if at % every == 0 and len(query_copies) <= 2 * steps:
            advance_query()
        order = order_of(chunk)
        copies[step - 1, chunk].wait()
        add(grads[chunk], lands[chunk], order, step - 1, rows)
        if step < steps:
            send(step, chunk)
        else:
            out_ref = (exp_ref, red_ref)[chunk // per_matrix]
            first = chunk % per_matrix * CHUNK
            out_ref[:, first:first + CHUNK] = grads[chunk][
                pl.ds(pl.multiple_of(place_of(me, order) * rows, rows), rows), :
            ]
    while len(query_copies) <= 2 * steps:
        advance_query()


def summed_grads(count, tile_rows, dpre_mid, dout, hidden_act, query_terms):
    width = tile_rows.shape[1]
    middle = hidden_act.shape[1]
    orders = bit_orders(count)
    steps = len(orders[0])
    chunks = 2 * middle // CHUNK
    queries = query_terms.shape[0]
    flat = query_terms.reshape(queries // 8, 8, width // 128, 128).transpose(0, 2, 1, 3)
    flat = flat.reshape(-1, 128)
    vmem = pl.BlockSpec(memory_space=pltpu.VMEM)
    red, exp, shared = pl.pallas_call(
        functools.partial(reduce_kernel, count, orders),
        out_shape=(
            jax.ShapeDtypeStruct((width // count, middle), jnp.float32),
            jax.ShapeDtypeStruct((width // count, middle), jnp.float32),
            jax.ShapeDtypeStruct(flat.shape, jnp.float32),
        ),
        in_specs=[vmem] * 5,
        out_specs=(vmem, vmem, vmem),
        scratch_shapes=(
            [pltpu.VMEM((width, CHUNK), jnp.float32)] * (2 * chunks)
            + [
                pltpu.VMEM(flat.shape, jnp.float32),
                pltpu.VMEM(flat.shape, jnp.float32),
                pltpu.SemaphoreType.DMA((steps, chunks)),
                pltpu.SemaphoreType.DMA((steps, chunks)),
                pltpu.SemaphoreType.DMA((2 * steps,)),
                pltpu.SemaphoreType.DMA((2 * steps,)),
            ]
        ),
        compiler_params=pltpu.CompilerParams(
            collective_id=0, has_side_effects=True, vmem_limit_bytes=56 * 1024 * 1024
        ),
    )(tile_rows, dpre_mid, dout, hidden_act, flat)
    shared = shared.reshape(queries // 8, width // 128, 8, 128).transpose(0, 2, 1, 3)
    return red, exp, shared.reshape(queries, width)


def on_device(count, tiles, slide_of, valid_count, labels, w_reduce, w_expand, queries, cls_weight):
    count_tiles, positions, width = tiles.shape
    slides = labels.shape[0]
    tile_rows = tiles.reshape(-1, width)
    pre_mid = jnp.dot(tile_rows, w_reduce, preferred_element_type=jnp.float32)
    hidden_act = jax.nn.silu(pre_mid).astype(jnp.bfloat16)
    pre_out = tile_rows.astype(jnp.float32) + jnp.dot(
        hidden_act, w_expand, preferred_element_type=jnp.float32
    )
    embed = jax.nn.silu(pre_out).reshape(count_tiles, positions, width).mean(axis=1)
    valid = jnp.arange(count_tiles) < valid_count[0]
    member = ((slide_of[:, None] == jnp.arange(slides)[None, :]) & valid[:, None]).astype(
        jnp.float32
    )
    query_vals = queries.astype(jnp.float32)
    class_vals = cls_weight.astype(jnp.float32)
    inv_root = 1.0 / jnp.sqrt(jnp.float32(width))
    count_queries = query_vals.shape[0]
    both_vals = jnp.concatenate([query_vals * inv_root, class_vals], axis=0)
    both = jnp.dot(embed, both_vals.T, precision=HIGH)
    scores = both[:, :count_queries]
    class_dot = both[:, count_queries:]
    of_slide = member[:, :, None]

    def per_tile(slide_vals):
        return jnp.sum(of_slide * slide_vals[None], axis=1)

    local_top = jnp.max(jnp.where(of_slide > 0, scores[:, None, :], -1e30), axis=0)
    local_weights = jnp.where(
        valid[:, None], jnp.exp(jnp.where(valid[:, None], scores - per_tile(local_top), 0.0)), 0.0
    )
    part_totals = jnp.sum(of_slide * local_weights[:, None, :], axis=0)
    part_dots = jnp.sum(of_slide * (local_weights * class_dot)[:, None, :], axis=0)
    gathered = gather_parts(count, jnp.concatenate([local_top, part_totals, part_dots]))
    gathered = gathered.reshape(count, 3, slides, count_queries)
    top_scores = jnp.max(gathered[:, 0], axis=0)
    rescale = jnp.exp(gathered[:, 0] - top_scores[None])
    totals = jnp.sum(rescale * gathered[:, 1], axis=0)
    ratio = jnp.sum(rescale * gathered[:, 2], axis=0) / totals
    logit = jnp.sum(ratio, axis=1)
    targets = labels.astype(jnp.float32)
    slide_loss = jax.nn.softplus(logit) - targets * logit
    dlogit = (jax.nn.sigmoid(logit) - targets) / slides
    weights = jnp.where(
        valid[:, None], jnp.exp(jnp.where(valid[:, None], scores - per_tile(top_scores), 0.0)), 0.0
    )
    prob = weights / jnp.where(valid[:, None], per_tile(totals), 1.0)
    prob_grad = prob * jnp.sum(member * dlogit[None], axis=1)[:, None]
    dscore = prob_grad * (class_dot - per_tile(ratio))
    dembed = jnp.dot(
        jnp.concatenate([dscore, prob_grad], axis=1), both_vals, precision=HIGH
    )
    query_terms = jnp.dot(dscore.T, embed, precision=HIGH) * inv_root
    dout = slope(pre_out).reshape(count_tiles, positions, width) * (dembed[:, None, :] / positions)
    dout = dout.reshape(-1, width).astype(jnp.bfloat16)
    dmid = jnp.dot(dout, w_expand.T, preferred_element_type=jnp.float32)
    dpre_mid = (dmid * slope(pre_mid)).astype(jnp.bfloat16)
    d_reduce, d_expand_t, d_queries = summed_grads(
        count, tile_rows, dpre_mid, dout, hidden_act, query_terms
    )
    return (slide_loss, d_queries, d_reduce, d_expand_t)


def solution(mesh):
    return jax.shard_map(
        functools.partial(on_device, mesh.shape["tile"]),
        mesh=mesh,
        in_specs=(
            P(("groups", "tile"), None, None),
            P(("groups", "tile")),
            P(("groups", "tile")),
            P("groups"),
            P(),
            P(),
            P(),
            P(),
        ),
        out_specs=(
            P("groups"),
            P("groups", None),
            P(("groups", "tile"), None),
            P(("groups", "tile"), None),
        ),
        check_vma=False,
    )
```

```python
import functools

import jax
import jax.numpy as jnp
from jax import lax
from jax.experimental import pallas as pl
from jax.experimental.pallas import tpu as pltpu
from jax.sharding import PartitionSpec as P

HIGH = lax.Precision.HIGHEST


def slope(values):
    sig = jax.nn.sigmoid(values)
    return sig * (1.0 + values * (1.0 - sig))


CHUNK = 128
LAG = 5
KINDS = (0, 1, 2, 0, 1, 2, 0, 1)


def bit_orders(count):
    bits = count.bit_length() - 1
    ring = list(range(1, bits))
    if bits != 5:
        return [[0] + ring[r:] + ring[:r] for r in (0, 1, 2)]
    return [[0, 1, 2, 3, 4], [0, 2, 1, 3, 4], [0, 3, 4, 1, 2]]


def gather_kernel(count, part_ref, all_ref, send_sem, recv_sem):
    me = lax.axis_index("tile")
    barrier = pltpu.get_barrier_semaphore()

    @pl.loop(1, count)
    def _(hop):
        pl.semaphore_signal(barrier, inc=1, device_id={"tile": lax.rem(me + hop, count)},
                            device_id_type=pl.DeviceIdType.MESH)

    all_ref[me] = part_ref[...]
    pl.semaphore_wait(barrier, count - 1)

    def copy_of(hop, slot):
        return pltpu.make_async_remote_copy(
            src_ref=part_ref, dst_ref=all_ref.at[slot],
            send_sem=send_sem.at[hop], recv_sem=recv_sem.at[hop],
            device_id={"tile": lax.rem(me + hop, count)},
            device_id_type=pl.DeviceIdType.MESH,
        )

    @pl.loop(1, count)
    def _(hop):
        copy_of(hop, me).start()

    @pl.loop(1, count)
    def _(hop):
        copy_of(hop, lax.rem(me - hop + count, count)).wait_recv()

    @pl.loop(1, count)
    def _(hop):
        copy_of(hop, me).wait_send()


def gather_parts(count, part):
    vmem = pl.BlockSpec(memory_space=pltpu.VMEM)
    rows, lanes = part.shape
    padded = jnp.pad(part, ((0, -rows % 8), (0, -lanes % 128)))
    return pl.pallas_call(
        functools.partial(gather_kernel, count),
        out_shape=jax.ShapeDtypeStruct((count,) + padded.shape, jnp.float32),
        in_specs=[vmem],
        out_specs=vmem,
        scratch_shapes=[pltpu.SemaphoreType.DMA((count,)), pltpu.SemaphoreType.DMA((count,))],
        compiler_params=pltpu.CompilerParams(collective_id=1, has_side_effects=True),
    )(padded)[:, :rows, :lanes]


def place_of(block, order):
    place = 0
    for bit in order:
        place = place * 2 + (block // (1 << bit)) % 2
    return place


def reduce_kernel(count, orders, tiles_ref, dmid_ref, dout_ref, hidden_ref, query_ref,
                  red_ref, exp_ref, query_out_ref, *scratch):
    per_matrix = hidden_ref.shape[1] // CHUNK
    chunks = 2 * per_matrix
    grads = scratch[:chunks]
    lands = scratch[chunks:2 * chunks]
    query_sum, query_land, send_sem, recv_sem, query_send, query_recv = scratch[2 * chunks:]
    steps = len(orders[0])
    me = lax.axis_index("tile")
    rows = tiles_ref.shape[1] // count
    query_rows = query_ref.shape[0] // count

    partners = [me + (1 << bit) * (1 - 2 * ((me // (1 << bit)) % 2)) for bit in range(steps)]
    barrier = pltpu.get_barrier_semaphore()
    for bit in range(steps):
        pl.semaphore_signal(barrier, inc=1, device_id={"tile": partners[bit]},
                            device_id_type=pl.DeviceIdType.MESH)
    pl.semaphore_wait(barrier, steps)

    def span(order, step, unit):
        half = count >> (step + 1)
        base = 0
        for at in range(step):
            base = base + ((me // (1 << order[at])) % 2) * (count >> (at + 1))
        mine = (me // (1 << order[step])) % 2
        keep = pl.multiple_of((base + mine * half) * unit, unit)
        give = pl.multiple_of((base + (1 - mine) * half) * unit, unit)
        return keep, give, half * unit

    def land_at(step, unit):
        return (count - (count >> step)) * unit

    def begin(source, land, order, step, unit, sends, recvs):
        keep, give, size = span(order, step, unit)
        copy = pltpu.make_async_remote_copy(
            src_ref=source.at[pl.ds(give, size)],
            dst_ref=land.at[pl.ds(land_at(step, unit), size)],
            send_sem=sends, recv_sem=recvs,
            device_id={"tile": partners[order[step]]},
            device_id_type=pl.DeviceIdType.MESH,
        )
        copy.start()
        return copy

    def add(source, land, order, step, unit):
        keep, give, size = span(order, step, unit)
        piece = min(size, 256)

        @pl.loop(0, size // piece)
        def _(at):
            here = pl.ds(pl.multiple_of(keep + at * piece, piece), piece)
            there = pl.ds(pl.multiple_of(land_at(step, unit) + at * piece, piece), piece)
            source[here, :] = source[here, :] + land[there, :]

    query_order = orders[0]
    query_sum[...] = query_ref[...]
    query_copies = [begin(query_sum, query_land, query_order, 0, query_rows,
                          query_send.at[0], query_recv.at[0])]

    def share(step):
        keep, give, size = span(query_order, step, query_rows)
        held = query_out_ref.at[pl.ds(keep, size)]
        copy = pltpu.make_async_remote_copy(
            src_ref=held, dst_ref=held,
            send_sem=query_send.at[steps + step], recv_sem=query_recv.at[steps + step],
            device_id={"tile": partners[query_order[step]]},
            device_id_type=pl.DeviceIdType.MESH,
        )
        copy.start()
        return copy

    def advance_query():
        done = len(query_copies) - 1
        query_copies[done].wait()
        if done < steps:
            add(query_sum, query_land, query_order, done, query_rows)
        if done < steps - 1:
            query_copies.append(begin(query_sum, query_land, query_order, done + 1, query_rows,
                                      query_send.at[done + 1], query_recv.at[done + 1]))
            return
        if done == steps - 1:
            own = pl.ds(pl.multiple_of(place_of(me, query_order) * query_rows, query_rows),
                        query_rows)
            query_out_ref[own, :] = query_sum[own, :]
        query_copies.append(share(2 * steps - 2 - done) if done < 2 * steps - 1 else None)

    def order_of(chunk):
        return orders[KINDS[chunk % len(KINDS)]]

    copies = {}

    def send(step, chunk):
        copies[step, chunk] = begin(grads[chunk], lands[chunk], order_of(chunk), step, rows,
                                    send_sem.at[step, chunk], recv_sem.at[step, chunk])

    wide = 256
    per_wide = wide // rows
    for matrix, (left_ref, right_ref) in enumerate(((dout_ref, hidden_ref), (tiles_ref, dmid_ref))):

        @pl.loop(0, tiles_ref.shape[1] // wide)
        def _(at):
            product = lax.dot_general(
                left_ref[:, pl.ds(pl.multiple_of(at * wide, wide), wide)],
                right_ref[...],
                (((0,), (0,)), ((), ())),
                preferred_element_type=jnp.float32,
            )
            for inner in range(per_wide):
                for kind in range(len(orders)):
                    place = place_of(at * per_wide + inner, orders[kind])
                    there = pl.ds(pl.multiple_of(place * rows, rows), rows)
                    for part in range(per_matrix):
                        if KINDS[part % len(KINDS)] == kind:
                            grads[matrix * per_matrix + part][there, :] = product[
                                inner * rows:(inner + 1) * rows, part * CHUNK:(part + 1) * CHUNK
                            ]

        for part in range(per_matrix):
            send(0, matrix * per_matrix + part)

    visits = sorted(
        ((step, chunk) for step in range(1, steps + 1) for chunk in range(chunks)),
        key=lambda visit: (visit[1] + LAG * visit[0], visit[1]),
    )
    every = len(visits) // (2 * steps)
    for at, (step, chunk) in enumerate(visits):
        if at % every == 0 and len(query_copies) <= 2 * steps:
            advance_query()
        order = order_of(chunk)
        copies[step - 1, chunk].wait()
        add(grads[chunk], lands[chunk], order, step - 1, rows)
        if step < steps:
            send(step, chunk)
        else:
            out_ref = (exp_ref, red_ref)[chunk // per_matrix]
            first = chunk % per_matrix * CHUNK
            out_ref[:, first:first + CHUNK] = grads[chunk][
                pl.ds(pl.multiple_of(place_of(me, order) * rows, rows), rows), :
            ]
    while len(query_copies) <= 2 * steps:
        advance_query()


def summed_grads(count, tile_rows, dpre_mid, dout, hidden_act, query_terms):
    width = tile_rows.shape[1]
    middle = hidden_act.shape[1]
    orders = bit_orders(count)
    steps = len(orders[0])
    chunks = 2 * middle // CHUNK
    queries = query_terms.shape[0]
    flat = query_terms.reshape(queries // 8, 8, width // 128, 128).transpose(0, 2, 1, 3)
    flat = flat.reshape(-1, 128)
    vmem = pl.BlockSpec(memory_space=pltpu.VMEM)
    red, exp, shared = pl.pallas_call(
        functools.partial(reduce_kernel, count, orders),
        out_shape=(
            jax.ShapeDtypeStruct((width // count, middle), jnp.float32),
            jax.ShapeDtypeStruct((width // count, middle), jnp.float32),
            jax.ShapeDtypeStruct(flat.shape, jnp.float32),
        ),
        in_specs=[vmem] * 5,
        out_specs=(vmem, vmem, vmem),
        scratch_shapes=(
            [pltpu.VMEM((width, CHUNK), jnp.float32)] * (2 * chunks)
            + [
                pltpu.VMEM(flat.shape, jnp.float32),
                pltpu.VMEM(flat.shape, jnp.float32),
                pltpu.SemaphoreType.DMA((steps, chunks)),
                pltpu.SemaphoreType.DMA((steps, chunks)),
                pltpu.SemaphoreType.DMA((2 * steps,)),
                pltpu.SemaphoreType.DMA((2 * steps,)),
            ]
        ),
        compiler_params=pltpu.CompilerParams(
            collective_id=0, has_side_effects=True, vmem_limit_bytes=56 * 1024 * 1024
        ),
    )(tile_rows, dpre_mid, dout, hidden_act, flat)
    shared = shared.reshape(queries // 8, width // 128, 8, 128).transpose(0, 2, 1, 3)
    return red, exp, shared.reshape(queries, width)


def on_device(count, tiles, slide_of, valid_count, labels, w_reduce, w_expand, queries, cls_weight):
    count_tiles, positions, width = tiles.shape
    slides = labels.shape[0]
    tile_rows = tiles.reshape(-1, width)
    pre_mid = jnp.dot(tile_rows, w_reduce, preferred_element_type=jnp.float32)
    hidden_act = jax.nn.silu(pre_mid).astype(jnp.bfloat16)
    pre_out = tile_rows.astype(jnp.float32) + jnp.dot(
        hidden_act, w_expand, preferred_element_type=jnp.float32
    )
    embed = jax.nn.silu(pre_out).reshape(count_tiles, positions, width).mean(axis=1)
    valid = jnp.arange(count_tiles) < valid_count[0]
    member = ((slide_of[:, None] == jnp.arange(slides)[None, :]) & valid[:, None]).astype(
        jnp.float32
    )
    query_vals = queries.astype(jnp.float32)
    class_vals = cls_weight.astype(jnp.float32)
    inv_root = 1.0 / jnp.sqrt(jnp.float32(width))
    count_queries = query_vals.shape[0]
    both_vals = jnp.concatenate([query_vals * inv_root, class_vals], axis=0)
    both = jnp.dot(embed, both_vals.T, precision=HIGH)
    scores = both[:, :count_queries]
    class_dot = both[:, count_queries:]
    of_slide = member[:, :, None]

    def per_tile(slide_vals):
        return jnp.sum(of_slide * slide_vals[None], axis=1)

    local_top = jnp.max(jnp.where(of_slide > 0, scores[:, None, :], -1e30), axis=0)
    local_weights = jnp.where(
        valid[:, None], jnp.exp(jnp.where(valid[:, None], scores - per_tile(local_top), 0.0)), 0.0
    )
    part_totals = jnp.sum(of_slide * local_weights[:, None, :], axis=0)
    part_dots = jnp.sum(of_slide * (local_weights * class_dot)[:, None, :], axis=0)
    packed = jnp.block([[local_top, part_totals], [part_dots, jnp.zeros_like(part_dots)]])
    gathered = gather_parts(count, packed)
    all_tops = gathered[:, :slides, :count_queries]
    all_totals = gathered[:, :slides, count_queries:]
    all_dots = gathered[:, slides:, :count_queries]
    top_scores = jnp.max(all_tops, axis=0)
    rescale = jnp.exp(all_tops - top_scores[None])
    totals = jnp.sum(rescale * all_totals, axis=0)
    ratio = jnp.sum(rescale * all_dots, axis=0) / totals
    logit = jnp.sum(ratio, axis=1)
    targets = labels.astype(jnp.float32)
    slide_loss = jax.nn.softplus(logit) - targets * logit
    dlogit = (jax.nn.sigmoid(logit) - targets) / slides
    weights = jnp.where(
        valid[:, None], jnp.exp(jnp.where(valid[:, None], scores - per_tile(top_scores), 0.0)), 0.0
    )
    prob = weights / jnp.where(valid[:, None], per_tile(totals), 1.0)
    prob_grad = prob * jnp.sum(member * dlogit[None], axis=1)[:, None]
    dscore = prob_grad * (class_dot - per_tile(ratio))
    dembed = jnp.dot(
        jnp.concatenate([dscore, prob_grad], axis=1), both_vals, precision=HIGH
    )
    query_terms = jnp.dot(dscore.T, embed, precision=HIGH) * inv_root
    dout = slope(pre_out).reshape(count_tiles, positions, width) * (dembed[:, None, :] / positions)
    dout = dout.reshape(-1, width).astype(jnp.bfloat16)
    dmid = jnp.dot(dout, w_expand.T, preferred_element_type=jnp.float32)
    dpre_mid = (dmid * slope(pre_mid)).astype(jnp.bfloat16)
    d_reduce, d_expand_t, d_queries = summed_grads(
        count, tile_rows, dpre_mid, dout, hidden_act, query_terms
    )
    return (slide_loss, d_queries, d_reduce, d_expand_t)


def solution(mesh):
    return jax.shard_map(
        functools.partial(on_device, mesh.shape["tile"]),
        mesh=mesh,
        in_specs=(
            P(("groups", "tile"), None, None),
            P(("groups", "tile")),
            P(("groups", "tile")),
            P("groups"),
            P(),
            P(),
            P(),
            P(),
        ),
        out_specs=(
            P("groups"),
            P("groups", None),
            P(("groups", "tile"), None),
            P(("groups", "tile"), None),
        ),
        check_vma=False,
    )
```
